32 devices in a mesh: segment: 4 (over z), ctx: 2 (over x), dp: 4 (over y, core).
Axes of the slice: x: 2, y: 2, z: 4, core: 2. Of those that a mesh axis runs over, the one named last changes fastest.
Arguments:
- qkv: bfloat16 [4, 4, 320, 3, 2560], P('segment', 'dp', 'ctx'), may hold values from -24 to 24
- qk_gain: float32 [4, 2, 2560], P('segment'), may hold values from 1.5 to 2.5
- mod_weight: float32 [4, 256, 2560], P('segment'), may hold values from -0.375 to 0.375
- positions: int32 [4, 320], P('dp', 'ctx'), may hold values from 0 to 75599
- timesteps: int32 [4, 4], P('segment', 'dp'), may hold values from 0 to 999
- cotangent: bfloat16 [4, 4, 320, 2560], P('segment', 'dp', 'ctx'), may hold values from -6 to 6
Outputs:
- attn_out: bfloat16 [4, 4, 320, 2560], P('segment', 'dp', 'ctx')
- gate_grad: float32 [4, 256, 2560], P('segment', ('ctx', 'dp'))
The draws below stay inside these ranges and needn't reach their ends.
All inputs are finite; a program needn't handle non-finite values.
Results may differ from the reference program's by a relative error of at most 0.012.
Values may be sent and summed in bfloat16 or wider, within the bound.
A program may use at most 128 MiB of HBM per device.

```python
import jax
import jax.numpy as jnp
from jax import lax

HEADS = 20
HEAD_DIM = 128
FREQS = 256
GRID_ROWS = 45
GRID_COLS = 80
FRAMES = 21
STEPS = 1000
TOKENS = 320
HW = 2560
N_SEGMENT = 4
N_DP = 4


def draw_qkv(key, part):
    width = HEADS * HEAD_DIM
    shape = (N_SEGMENT, N_DP, TOKENS, 3, width)
    streams = jax.random.split(jax.random.fold_in(key, 11), 1)
    base = jax.random.normal(streams[0], shape, jnp.float32)
    return jnp.clip(base, -24.0, 24.0).astype(jnp.bfloat16)


def with_ends(values, key, low, largest):
    index_at = [jax.random.randint(jax.random.fold_in(key, axis), (), 0, length) for axis, length in enumerate(values.shape)]
    main_axis = values.shape.index(max(values.shape))
    next_to = index_at[:main_axis] + [(index_at[main_axis] + 1) % values.shape[main_axis]] + index_at[main_axis + 1:]
    return values.at[tuple(index_at)].set(low).at[tuple(next_to)].set(largest)


def shard_levels(stream_key, shape, shards, least, high):
    level, own = 1.0, jax.random.fold_in(stream_key, 6)
    for axis_at, parts in shards:
        heights = jnp.exp(jax.random.uniform(jax.random.fold_in(own, axis_at), (parts,), jnp.float32, least / len(shards), high / len(shards)))
        level = level * jnp.repeat(heights, shape[axis_at] // parts).reshape([-1 if axis == axis_at else 1 for axis in range(len(shape))])
    return level


def bell_draw(key, extent, scale, most, cuts=(), kind=jnp.bfloat16):
    values = jax.random.normal(key, extent, jnp.float32) * scale
    if len(cuts) > 0:
        values = shard_levels(key, extent, cuts, -0.22, 0.18) * values
    return jnp.clip(values, min=-most, max=most).astype(kind)


def setup_inputs(seed: int = 0) -> dict:
    arg_keys = jax.random.split(jax.random.key(seed), 7)
    qkv = draw_qkv(jax.random.fold_in(arg_keys[6], 71), 0)
    qk_gain = jnp.clip(1.5 + 1.0 * jax.random.uniform(arg_keys[1], (N_SEGMENT, 2, HW), jnp.float32) ** shard_levels(arg_keys[1], (N_SEGMENT, 2, HW), ((0, 4),), -0.2, 0.2), 1.5, 2.5)
    mod_weight = bell_draw(arg_keys[2], (N_SEGMENT, FREQS, HW), FREQS ** -0.5, 0.375, ((0, 4),), jnp.float32)
    positions = with_ends(jax.random.randint(arg_keys[3], (N_DP, TOKENS), 0, FRAMES * GRID_ROWS * GRID_COLS), jax.random.fold_in(arg_keys[3], 1), 0, (FRAMES * GRID_ROWS * GRID_COLS) - 1).astype(jnp.int32)
    timesteps = with_ends(jax.random.randint(arg_keys[4], (N_SEGMENT, N_DP), 0, STEPS), jax.random.fold_in(arg_keys[4], 1), 0, STEPS - 1).astype(jnp.int32)
    cotangent = bell_draw(arg_keys[5], (N_SEGMENT, N_DP, TOKENS, HW), 1.0, 6.0, ((0, 4), (1, 4), (2, 2)))
    return {"qkv": qkv, "qk_gain": qk_gain, "mod_weight": mod_weight, "positions": positions, "timesteps": timesteps, "cotangent": cotangent}


def rope_tables(pos):
    half = HEAD_DIM // 2
    side = HEAD_DIM // 6
    first = half - 2 * side
    frame = (pos // (GRID_ROWS * GRID_COLS)).astype(jnp.float32)
    row = (pos // GRID_COLS % GRID_ROWS).astype(jnp.float32)
    col = (pos % GRID_COLS).astype(jnp.float32)
    pair = jnp.arange(half, dtype=jnp.int32)
    group = jnp.where(pair < first, 0, jnp.where(pair < first + side, 1, 2))
    offset = jnp.where(group == 0, 0, jnp.where(group == 1, first, first + side))
    pairs_in = jnp.where(group == 0, first, side).astype(jnp.float32)
    freq = 10000.0 ** (-(pair - offset).astype(jnp.float32) / pairs_in)
    coord = jnp.where(group[None, :] == 0, frame[:, None], jnp.where(group[None, :] == 1, row[:, None], col[:, None]))
    angle = coord * freq[None, :]
    cosine = jnp.tile(jnp.concatenate([jnp.cos(angle), jnp.cos(angle)], axis=1), (1, HEADS))
    sine = jnp.tile(jnp.concatenate([jnp.sin(angle), jnp.sin(angle)], axis=1), (1, HEADS))
    return (cosine, sine)

def rotate(values, cosine, sine):
    count = values.shape[0]
    half = HEAD_DIM // 2
    shaped = values.reshape(count, HEADS, HEAD_DIM)
    turned = jnp.concatenate([-shaped[:, :, half:], shaped[:, :, :half]], axis=2).reshape(count, HEADS * HEAD_DIM)
    return values * cosine + turned * sine

def normalize(values, gain):
    mean_sq = lax.optimization_barrier(jnp.mean(values * values, axis=-1, keepdims=True))
    return values * lax.rsqrt(mean_sq + 1e-06) * gain

def embed(step):
    count = FREQS // 2
    freq = 10000.0 ** (-jnp.arange(count, dtype=jnp.float32) / count)
    angle = step.astype(jnp.float32) * freq
    return jnp.concatenate([jnp.cos(angle), jnp.sin(angle)])

def attention(queries, keys, values):
    count = queries.shape[0]
    qh = queries.astype(jnp.float32).reshape(count, HEADS, HEAD_DIM).transpose(1, 0, 2)
    kh = keys.astype(jnp.float32).reshape(count, HEADS, HEAD_DIM).transpose(1, 0, 2)
    vh = values.astype(jnp.float32).reshape(count, HEADS, HEAD_DIM).transpose(1, 0, 2)
    scale = 1.0 / HEAD_DIM ** 0.5

    def one_head(operands):
        qone, kone, vone = operands
        scores = jnp.dot(qone, kone.T, precision=lax.Precision.HIGHEST) * scale
        peak = lax.optimization_barrier(jnp.max(scores, axis=1, keepdims=True))
        expo = jnp.exp(scores - peak)
        total = lax.optimization_barrier(jnp.sum(expo, axis=1, keepdims=True))
        rounded = expo.astype(jnp.bfloat16).astype(jnp.float32)
        return jnp.dot(rounded, vone, precision=lax.Precision.HIGHEST) / total
    result = lax.map(one_head, (qh, kh, vh))
    return result.transpose(1, 0, 2).reshape(count, HEADS * HEAD_DIM)

def reference(qkv, qk_gain, mod_weight, positions, timesteps, cotangent):
    source = jnp.roll(qkv, 1, axis=0)
    outs = []
    grads = []
    for segment_idx in range(N_SEGMENT):
        segment_outs = []
        grad_sum = jnp.zeros((FREQS, HEADS * HEAD_DIM), jnp.float32)
        for clip_idx in range(N_DP):
            block = source[segment_idx, clip_idx].astype(jnp.float32)
            cosine, sine = rope_tables(positions[clip_idx])
            queries = rotate(normalize(block[:, 0], qk_gain[segment_idx, 0]), cosine, sine).astype(jnp.bfloat16)
            keys = rotate(normalize(block[:, 1], qk_gain[segment_idx, 1]), cosine, sine).astype(jnp.bfloat16)
            values = source[segment_idx, clip_idx, :, 2]
            attn = attention(queries, keys, values)
            emb = embed(timesteps[segment_idx, clip_idx])
            gate = jnp.dot(emb, mod_weight[segment_idx], precision=lax.Precision.HIGHEST)
            segment_outs.append((attn * gate).astype(jnp.bfloat16))
            chan = lax.optimization_barrier(jnp.sum(attn * cotangent[segment_idx, clip_idx].astype(jnp.float32), axis=0))
            grad_sum = grad_sum + emb[:, None] * chan[None, :]
        outs.append(jnp.stack(segment_outs))
        grads.append(grad_sum)
    return (jnp.stack(outs), jnp.stack(grads))
```

```python
import functools
import math

import jax
import jax.numpy as jnp
import numpy as np
from jax import lax
from jax.experimental import pallas as pl
from jax.experimental.pallas import tpu as pltpu
from jax.sharding import PartitionSpec as P

HEAD_DIM = 128
GRID_ROWS = 45
GRID_COLS = 80
MESH = pl.DeviceIdType.MESH
LEAD = 8
LAG = 4


def sincos(angle):
    turns = jnp.floor(angle * (2.0 / math.pi) + 0.5)
    quad = turns.astype(jnp.int32)
    r = angle - turns * 1.5703125
    r = r - turns * 4.837512969970703125e-4
    r = r - turns * 7.549789948768648e-8
    z = r * r
    sine = r + r * z * (-1.6666654611e-1 + z * (8.3321608736e-3 - z * 1.9515295891e-4))
    cosine = 1.0 - 0.5 * z + z * z * (
        4.166664568298827e-2 + z * (-1.388731625493765e-3 + z * 2.443315711809948e-5)
    )
    swap = (quad & 1) == 1
    s = jnp.where(swap, cosine, sine)
    c = jnp.where(swap, sine, cosine)
    s = jnp.where((quad & 2) == 2, -s, s)
    c = jnp.where(((quad + 1) & 2) == 2, -c, c)
    return s, c


def rope_freqs():
    half = HEAD_DIM // 2
    side = HEAD_DIM // 6
    first = half - 2 * side
    rows = np.zeros((8, HEAD_DIM), np.float64)
    start = 0
    for group, count in enumerate((first, side, side)):
        for j in range(count):
            for lane in (start + j, start + j + half):
                rows[group, lane] = 10000.0 ** (-j / count)
        start += count
    return rows.astype(np.float32)


def body(
    S, C, D, heads, freqs,
    x_ref, gain_ref, w_ref, pos_ref, t_ref, cot_ref, freq_ref,
    out_ref, grad_ref,
    xv, wv, cotv, kv, qbuf, abuf, rbuf, gains, tbuf, ebuf, cbuf, gate, cosv, sinv,
    load_sem, kv_send, kv_recv, a_send, a_recv, g_send, g_recv, t_send, t_recv, c_send, c_recv,
):
    n = C * D
    count = x_ref.shape[1]
    rows = freqs // n
    hd = HEAD_DIM
    seg = lax.axis_index("segment")
    ctx = lax.axis_index("ctx")
    dp = lax.axis_index("dp")
    me = ctx * D + dp
    after = {"segment": lax.rem(seg + 1, S)}
    before = {"segment": lax.rem(seg + S - 1, S)}
    peers = []
    for r in range(1, n):
        p = lax.rem(me + r, n)
        peers.append({"ctx": p // D, "dp": lax.rem(p, D)})
    ring = [{"ctx": lax.rem(ctx + r, C)} for r in range(1, C)]

    def cols(h):
        return pl.ds(pl.multiple_of(h * hd, hd), hd)

    loads = [
        pltpu.make_async_copy(x_ref.at[1], xv.at[1], load_sem.at[1]),
        pltpu.make_async_copy(x_ref.at[0], xv.at[0], load_sem.at[0]),
        pltpu.make_async_copy(x_ref.at[2], xv.at[2], load_sem.at[2]),
        pltpu.make_async_copy(w_ref, wv, load_sem.at[3]),
        pltpu.make_async_copy(cot_ref, cotv, load_sem.at[4]),
    ]
    for load in loads:
        load.start()
    step = t_ref[0, 0].astype(jnp.float32)
    tbuf[0] = jnp.full((8, hd), step, jnp.float32)

    barrier = pltpu.get_barrier_semaphore()
    for who in peers + [after, before]:
        pl.semaphore_signal(barrier, inc=1, device_id=who, device_id_type=MESH)
    pl.semaphore_wait(barrier, n + 1)

    gain_copy = pltpu.make_async_remote_copy(
        src_ref=gain_ref, dst_ref=gains, send_sem=g_send, recv_sem=g_recv,
        device_id=before, device_id_type=MESH,
    )
    gain_copy.start()

    def send_values(h):
        for r in range(1, C):
            pltpu.make_async_remote_copy(
                src_ref=x_ref.at[2, :, cols(h)],
                dst_ref=kv.at[h, 1, pl.ds(r * count, count), :],
                send_sem=kv_send.at[h], recv_sem=kv_recv.at[h],
                device_id=ring[r - 1], device_id_type=MESH,
            ).start()

    def send_keys(h):
        for r in range(1, C):
            pltpu.make_async_remote_copy(
                src_ref=kv.at[h, 0, pl.ds(0, count), :],
                dst_ref=kv.at[h, 0, pl.ds(r * count, count), :],
                send_sem=kv_send.at[h], recv_sem=kv_recv.at[h],
                device_id=ring[r - 1], device_id_type=MESH,
            ).start()

    lead = min(LEAD, heads)

    @pl.loop(0, lead)
    def _(h):
        send_values(h)

    for r in range(1, n):
        pltpu.make_async_remote_copy(
            src_ref=tbuf.at[0], dst_ref=tbuf.at[r], send_sem=t_send, recv_sem=t_recv,
            device_id=peers[r - 1], device_id_type=MESH,
        ).start()

    pos = jnp.broadcast_to(pos_ref[...], (count, hd))
    frame = (pos // (GRID_ROWS * GRID_COLS)).astype(jnp.float32)
    row = (pos // GRID_COLS % GRID_ROWS).astype(jnp.float32)
    col = (pos % GRID_COLS).astype(jnp.float32)
    angle = frame * freq_ref[0:1, :] + row * freq_ref[1:2, :] + col * freq_ref[2:3, :]
    s, c = sincos(angle)
    lane = lax.broadcasted_iota(jnp.int32, (count, hd), 1)
    cosv[...] = c
    sinv[...] = jnp.where(lane < hd // 2, -s, s)

    def inverse_norm(which):
        def add(h, acc):
            x = xv[which, :, cols(h)].astype(jnp.float32)
            return acc + x * x

        total = lax.fori_loop(0, heads, add, jnp.zeros((count, hd), jnp.float32))
        mean = jnp.sum(total, axis=1, keepdims=True) / (heads * hd)
        return lax.rsqrt(mean + 1e-06)

    def turned(which, h, inv):
        x = xv[which, :, cols(h)].astype(jnp.float32)
        x = x * inv * gains[which : which + 1, cols(h)]
        return (x * cosv[...] + pltpu.roll(x, hd // 2, 1) * sinv[...]).astype(jnp.bfloat16)

    loads[0].wait()
    inv_k = inverse_norm(1)
    gain_copy.wait_recv()

    @pl.loop(0, heads)
    def _(h):
        kv[h, 0, 0:count, :] = turned(1, h, inv_k)
        send_keys(h)

        @pl.when(h + lead < heads)
        def _():
            send_values(h + lead)

    loads[1].wait()
    inv_q = inverse_norm(0)
    loads[2].wait()

    @pl.loop(0, heads)
    def _(h):
        qbuf[h] = turned(0, h, inv_q)
        kv[h, 1, 0:count, :] = xv[2, :, cols(h)]

    half = freqs // 2
    decay = -math.log(10000.0) / half
    index = lax.broadcasted_iota(jnp.int32, (half, hd), 0).astype(jnp.float32)
    es, ec = sincos(step * jnp.exp(index * decay))
    loads[3].wait()

    @pl.loop(0, heads)
    def _(h):
        part = wv[0:half, cols(h)] * ec + wv[half:freqs, cols(h)] * es
        gate[pl.ds(h, 1), :] = jnp.sum(part, axis=0, keepdims=True)

    if n > 1:
        pltpu.make_async_copy(tbuf.at[pl.ds(1, n - 1)], tbuf.at[pl.ds(1, n - 1)], t_recv).wait()
    at = lax.broadcasted_iota(jnp.int32, (rows, hd), 0) + me * rows
    freq = jnp.exp((at % half).astype(jnp.float32) * decay)
    for j in range(n):
        s, c = sincos(tbuf[j, 0:1, :] * freq)
        ebuf[j] = jnp.where(at < half, c, s)
    loads[4].wait()

    scale = 1.0 / hd**0.5

    def attend(h):
        arrived = kv.at[h, :, pl.ds(count, (C - 1) * count), :]
        pltpu.make_async_copy(arrived, arrived, kv_recv.at[h]).wait()
        scores = lax.dot_general(
            qbuf[h], kv[h, 0], (((1,), (1,)), ((), ())), preferred_element_type=jnp.float32
        ) * scale
        expo = jnp.exp(scores - jnp.max(scores, axis=1, keepdims=True))
        total = jnp.sum(expo, axis=1, keepdims=True)
        mixed = jnp.dot(expo.astype(jnp.bfloat16), kv[h, 1], preferred_element_type=jnp.float32)
        abuf[h] = (mixed / total).astype(jnp.bfloat16)
        pltpu.make_async_remote_copy(
            src_ref=abuf.at[h], dst_ref=rbuf.at[h], send_sem=a_send.at[h], recv_sem=a_recv.at[h],
            device_id=after, device_id_type=MESH,
        ).start()

    def finish(h):
        pltpu.make_async_copy(rbuf.at[h], rbuf.at[h], a_recv.at[h]).wait()
        attn = rbuf[h].astype(jnp.float32)
        out_ref[:, cols(h)] = (attn * gate[pl.ds(h, 1), :]).astype(jnp.bfloat16)
        cot = cotv[:, cols(h)].astype(jnp.float32)
        cbuf[0, pl.ds(h, 1), :] = jnp.sum(attn * cot, axis=0, keepdims=True)

    @pl.loop(0, heads)
    def _(h):
        attend(h)

        @pl.when(h >= LAG)
        def _():
            finish(h - LAG)

    @pl.loop(max(heads - LAG, 0), heads)
    def _(h):
        finish(h)

    for r in range(1, n):
        pltpu.make_async_remote_copy(
            src_ref=cbuf.at[0], dst_ref=cbuf.at[r], send_sem=c_send, recv_sem=c_recv,
            device_id=peers[r - 1], device_id_type=MESH,
        ).start()
    pltpu.make_async_copy(cbuf.at[pl.ds(1, n - 1)], cbuf.at[pl.ds(1, n - 1)], c_recv).wait()

    @pl.loop(0, heads)
    def _(h):
        acc = ebuf[0] * cbuf[0, pl.ds(h, 1), :]
        for j in range(1, n):
            acc = acc + ebuf[j] * cbuf[j, pl.ds(h, 1), :]
        grad_ref[:, cols(h)] = acc

    gain_copy.wait_send()
    pltpu.make_async_copy(tbuf.at[pl.ds(1, n - 1)], tbuf.at[pl.ds(1, n - 1)], t_send).wait()
    pltpu.make_async_copy(cbuf.at[pl.ds(1, n - 1)], cbuf.at[pl.ds(1, n - 1)], c_send).wait()

    @pl.loop(0, heads)
    def _(h):
        sent = kv.at[h, :, pl.ds(count, (C - 1) * count), :]
        pltpu.make_async_copy(sent, sent, kv_send.at[h]).wait()
        pltpu.make_async_copy(abuf.at[h], abuf.at[h], a_send.at[h]).wait()


def local(S, C, D, qkv, qk_gain, mod_weight, positions, timesteps, cotangent):
    count, _, width = qkv.shape[2:]
    freqs = mod_weight.shape[1]
    heads = width // HEAD_DIM
    n = C * D
    rows = freqs // n
    hd = HEAD_DIM
    padded = -(-heads // 8) * 8
    bf, f32 = jnp.bfloat16, jnp.float32
    vmem = pl.BlockSpec(memory_space=pltpu.VMEM)
    hbm = pl.BlockSpec(memory_space=pl.ANY)
    dma = pltpu.SemaphoreType.DMA
    attn_out, grad = pl.pallas_call(
        functools.partial(body, S, C, D, heads, freqs),
        out_shape=(
            jax.ShapeDtypeStruct((count, width), bf),
            jax.ShapeDtypeStruct((rows, width), f32),
        ),
        in_specs=[hbm, vmem, hbm, vmem, pl.BlockSpec(memory_space=pltpu.SMEM), hbm, vmem],
        out_specs=(vmem, vmem),
        scratch_shapes=[
            pltpu.VMEM((3, count, width), bf),
            pltpu.VMEM((freqs, width), f32),
            pltpu.VMEM((count, width), bf),
            pltpu.VMEM((heads, 2, C * count, hd), bf),
            pltpu.VMEM((heads, count, hd), bf),
            pltpu.VMEM((heads, count, hd), bf),
            pltpu.VMEM((heads, count, hd), bf),
            pltpu.VMEM((2, width), f32),
            pltpu.VMEM((n, 8, hd), f32),
            pltpu.VMEM((n, rows, hd), f32),
            pltpu.VMEM((n, padded, hd), f32),
            pltpu.VMEM((padded, hd), f32),
            pltpu.VMEM((count, hd), f32),
            pltpu.VMEM((count, hd), f32),
            dma((5,)),
            dma((heads,)), dma((heads,)), dma((heads,)), dma((heads,)),
            dma, dma, dma, dma, dma, dma,
        ],
        compiler_params=pltpu.CompilerParams(
            collective_id=0, has_side_effects=True, vmem_limit_bytes=60 << 20
        ),
    )(
        jnp.moveaxis(qkv[0, 0], 1, 0),
        qk_gain[0],
        mod_weight[0],
        positions.reshape(count, 1),
        timesteps,
        cotangent[0, 0],
        jnp.asarray(rope_freqs()),
    )
    return attn_out[None, None], grad[None]


def solution(mesh):
    sizes = mesh.shape
    return jax.shard_map(
        functools.partial(local, sizes["segment"], sizes["ctx"], sizes["dp"]),
        mesh=mesh,
        in_specs=(
            P("segment", "dp", "ctx", None, None),
            P("segment", None, None),
            P("segment", None, None),
            P("dp", "ctx"),
            P("segment", "dp"),
            P("segment", "dp", "ctx", None),
        ),
        out_specs=(P("segment", "dp", "ctx", None), P("segment", ("ctx", "dp"), None)),
        check_vma=False,
    )
```

```python
import functools
import math

import jax
import jax.numpy as jnp
from jax import lax
from jax.experimental import pallas as pl
from jax.experimental.pallas import tpu as pltpu
from jax.sharding import PartitionSpec as P

HEAD_DIM = 128
GRID_ROWS = 45
GRID_COLS = 80
MESH = pl.DeviceIdType.MESH
LEAD = 8
LAG = 4
VMEM_LIMIT = 24 << 20


def sincos(angle):
    turns = jnp.floor(angle * (2.0 / math.pi) + 0.5)
    quad = turns.astype(jnp.int32)
    r = angle - turns * 1.5703125
    r = r - turns * 4.837512969970703125e-4
    r = r - turns * 7.549789948768648e-8
    z = r * r
    sine = r + r * z * (-1.6666654611e-1 + z * (8.3321608736e-3 - z * 1.9515295891e-4))
    cosine = 1.0 - 0.5 * z + z * z * (
        4.166664568298827e-2 + z * (-1.388731625493765e-3 + z * 2.443315711809948e-5)
    )
    swap = (quad & 1) == 1
    s = jnp.where(swap, cosine, sine)
    c = jnp.where(swap, sine, cosine)
    s = jnp.where((quad & 2) == 2, -s, s)
    c = jnp.where(((quad + 1) & 2) == 2, -c, c)
    return s, c


def rope_angles(pos):
    count, hd = pos.shape
    half = hd // 2
    side = hd // 6
    first = half - 2 * side
    pair = lax.broadcasted_iota(jnp.int32, (8, hd), 1) % half
    group = jnp.where(pair < first, 0, jnp.where(pair < first + side, 1, 2))
    offset = jnp.where(group == 0, 0, jnp.where(group == 1, first, first + side))
    pairs_in = jnp.where(group == 0, first, side).astype(jnp.float32)
    freq = jnp.exp((pair - offset).astype(jnp.float32) / pairs_in * -math.log(10000.0))[0:1]
    group = group[0:1]
    frame = (pos // (GRID_ROWS * GRID_COLS)).astype(jnp.float32)
    row = (pos // GRID_COLS % GRID_ROWS).astype(jnp.float32)
    col = (pos % GRID_COLS).astype(jnp.float32)
    return jnp.where(group == 0, frame, jnp.where(group == 1, row, col)) * freq


def body(
    S, C, D, heads, freqs,
    x_ref, gain_ref, w_ref, pos_ref, t_ref, cot_ref,
    out_ref, grad_ref,
    xv, wv, cotv, kv, qbuf, abuf, rbuf, gains, tbuf, ebuf, cbuf, gate, cosv, sinv,
    load_sem, kv_send, kv_recv, a_send, a_recv, g_send, g_recv, t_send, t_recv, c_send, c_recv,
):
    n = C * D
    count = x_ref.shape[1]
    rows = freqs // n
    hd = HEAD_DIM
    seg = lax.axis_index("segment")
    ctx = lax.axis_index("ctx")
    dp = lax.axis_index("dp")
    me = ctx * D + dp
    after = {"segment": lax.rem(seg + 1, S)}
    before = {"segment": lax.rem(seg + S - 1, S)}
    peers = []
    for r in range(1, n):
        p = lax.rem(me + r, n)
        peers.append({"ctx": p // D, "dp": lax.rem(p, D)})
    ring = [{"ctx": lax.rem(ctx + r, C)} for r in range(1, C)]

    def cols(h):
        return pl.ds(pl.multiple_of(h * hd, hd), hd)

    loads = [
        pltpu.make_async_copy(x_ref.at[1], xv.at[1], load_sem.at[1]),
        pltpu.make_async_copy(x_ref.at[0], xv.at[0], load_sem.at[0]),
        pltpu.make_async_copy(x_ref.at[2], xv.at[2], load_sem.at[2]),
        pltpu.make_async_copy(w_ref, wv, load_sem.at[3]),
        pltpu.make_async_copy(cot_ref, cotv, load_sem.at[4]),
    ]
    for load in loads:
        load.start()
    step = t_ref[0, 0].astype(jnp.float32)
    tbuf[0] = jnp.full((8, hd), step, jnp.float32)

    barrier = pltpu.get_barrier_semaphore()
    for who in peers + [after, before]:
        pl.semaphore_signal(barrier, inc=1, device_id=who, device_id_type=MESH)
    pl.semaphore_wait(barrier, n + 1)

    gain_copy = pltpu.make_async_remote_copy(
        src_ref=gain_ref, dst_ref=gains, send_sem=g_send, recv_sem=g_recv,
        device_id=before, device_id_type=MESH,
    )
    gain_copy.start()

    def send_values(h):
        for r in range(1, C):
            pltpu.make_async_remote_copy(
                src_ref=x_ref.at[2, :, cols(h)],
                dst_ref=kv.at[h, 1, pl.ds(r * count, count), :],
                send_sem=kv_send.at[h], recv_sem=kv_recv.at[h],
                device_id=ring[r - 1], device_id_type=MESH,
            ).start()

    def send_keys(h):
        for r in range(1, C):
            pltpu.make_async_remote_copy(
                src_ref=kv.at[h, 0, pl.ds(0, count), :],
                dst_ref=kv.at[h, 0, pl.ds(r * count, count), :],
                send_sem=kv_send.at[h], recv_sem=kv_recv.at[h],
                device_id=ring[r - 1], device_id_type=MESH,
            ).start()

    lead = min(LEAD, heads)

    @pl.loop(0, lead)
    def _(h):
        send_values(h)

    for r in range(1, n):
        pltpu.make_async_remote_copy(
            src_ref=tbuf.at[0], dst_ref=tbuf.at[r], send_sem=t_send, recv_sem=t_recv,
            device_id=peers[r - 1], device_id_type=MESH,
        ).start()

    pos = jnp.transpose(jnp.broadcast_to(pos_ref[...], (hd, count)))
    s, c = sincos(rope_angles(pos))
    lane = lax.broadcasted_iota(jnp.int32, (count, hd), 1)
    cosv[...] = c
    sinv[...] = jnp.where(lane < hd // 2, -s, s)

    def inverse_norm(which):
        def add(h, acc):
            x = xv[which, :, cols(h)].astype(jnp.float32)
            return acc + x * x

        total = lax.fori_loop(0, heads, add, jnp.zeros((count, hd), jnp.float32))
        mean = jnp.sum(total, axis=1, keepdims=True) / (heads * hd)
        return lax.rsqrt(mean + 1e-06)

    def turned(which, h, inv):
        x = xv[which, :, cols(h)].astype(jnp.float32)
        x = x * inv * gains[which : which + 1, cols(h)]
        return (x * cosv[...] + pltpu.roll(x, hd // 2, 1) * sinv[...]).astype(jnp.bfloat16)

    loads[0].wait()
    inv_k = inverse_norm(1)
    gain_copy.wait_recv()

    @pl.loop(0, heads)
    def _(h):
        kv[h, 0, 0:count, :] = turned(1, h, inv_k)
        send_keys(h)

        @pl.when(h + lead < heads)
        def _():
            send_values(h + lead)

    loads[1].wait()
    inv_q = inverse_norm(0)
    loads[2].wait()

    @pl.loop(0, heads)
    def _(h):
        qbuf[h] = turned(0, h, inv_q)
        kv[h, 1, 0:count, :] = xv[2, :, cols(h)]

    half = freqs // 2
    decay = -math.log(10000.0) / half
    index = lax.broadcasted_iota(jnp.int32, (half, hd), 0).astype(jnp.float32)
    es, ec = sincos(step * jnp.exp(index * decay))
    loads[3].wait()

    @pl.loop(0, heads)
    def _(h):
        part = wv[0:half, cols(h)] * ec + wv[half:freqs, cols(h)] * es
        gate[pl.ds(h, 1), :] = jnp.sum(part, axis=0, keepdims=True)

    if n > 1:
        pltpu.make_async_copy(tbuf.at[pl.ds(1, n - 1)], tbuf.at[pl.ds(1, n - 1)], t_recv).wait()
    at = lax.broadcasted_iota(jnp.int32, (rows, hd), 0) + me * rows
    freq = jnp.exp((at % half).astype(jnp.float32) * decay)
    for j in range(n):
        s, c = sincos(tbuf[j, 0:1, :] * freq)
        ebuf[j] = jnp.where(at < half, c, s)
    loads[4].wait()

    scale = 1.0 / hd**0.5

    def attend(h):
        arrived = kv.at[h, :, pl.ds(count, (C - 1) * count), :]
        pltpu.make_async_copy(arrived, arrived, kv_recv.at[h]).wait()
        scores = lax.dot_general(
            qbuf[h], kv[h, 0], (((1,), (1,)), ((), ())), preferred_element_type=jnp.float32
        ) * scale
        expo = jnp.exp(scores - jnp.max(scores, axis=1, keepdims=True))
        total = jnp.sum(expo, axis=1, keepdims=True)
        mixed = jnp.dot(expo.astype(jnp.bfloat16), kv[h, 1], preferred_element_type=jnp.float32)
        abuf[h] = (mixed / total).astype(jnp.bfloat16)
        pltpu.make_async_remote_copy(
            src_ref=abuf.at[h], dst_ref=rbuf.at[h], send_sem=a_send.at[h], recv_sem=a_recv.at[h],
            device_id=after, device_id_type=MESH,
        ).start()

    def finish(h):
        pltpu.make_async_copy(rbuf.at[h], rbuf.at[h], a_recv.at[h]).wait()
        attn = rbuf[h].astype(jnp.float32)
        out_ref[:, cols(h)] = (attn * gate[pl.ds(h, 1), :]).astype(jnp.bfloat16)
        cot = cotv[:, cols(h)].astype(jnp.float32)
        cbuf[0, pl.ds(h, 1), :] = jnp.sum(attn * cot, axis=0, keepdims=True)

    @pl.loop(0, heads)
    def _(h):
        attend(h)

        @pl.when(h >= LAG)
        def _():
            finish(h - LAG)

    @pl.loop(max(heads - LAG, 0), heads)
    def _(h):
        finish(h)

    for r in range(1, n):
        pltpu.make_async_remote_copy(
            src_ref=cbuf.at[0], dst_ref=cbuf.at[r], send_sem=c_send, recv_sem=c_recv,
            device_id=peers[r - 1], device_id_type=MESH,
        ).start()
    pltpu.make_async_copy(cbuf.at[pl.ds(1, n - 1)], cbuf.at[pl.ds(1, n - 1)], c_recv).wait()

    @pl.loop(0, heads)
    def _(h):
        acc = ebuf[0] * cbuf[0, pl.ds(h, 1), :]
        for j in range(1, n):
            acc = acc + ebuf[j] * cbuf[j, pl.ds(h, 1), :]
        grad_ref[:, cols(h)] = acc

    gain_copy.wait_send()
    pltpu.make_async_copy(tbuf.at[pl.ds(1, n - 1)], tbuf.at[pl.ds(1, n - 1)], t_send).wait()
    pltpu.make_async_copy(cbuf.at[pl.ds(1, n - 1)], cbuf.at[pl.ds(1, n - 1)], c_send).wait()

    @pl.loop(0, heads)
    def _(h):
        sent = kv.at[h, :, pl.ds(count, (C - 1) * count), :]
        pltpu.make_async_copy(sent, sent, kv_send.at[h]).wait()
        pltpu.make_async_copy(abuf.at[h], abuf.at[h], a_send.at[h]).wait()


def local(S, C, D, qkv, qk_gain, mod_weight, positions, timesteps, cotangent):
    count, _, width = qkv.shape[2:]
    freqs = mod_weight.shape[1]
    heads = width // HEAD_DIM
    n = C * D
    rows = freqs // n
    hd = HEAD_DIM
    padded = -(-heads // 8) * 8
    bf, f32 = jnp.bfloat16, jnp.float32
    vmem = pl.BlockSpec(memory_space=pltpu.VMEM)
    hbm = pl.BlockSpec(memory_space=pltpu.HBM)
    dma = pltpu.SemaphoreType.DMA
    pin = functools.partial(pltpu.with_memory_space_constraint, memory_space=pltpu.HBM)
    attn_out, grad = pl.pallas_call(
        functools.partial(body, S, C, D, heads, freqs),
        out_shape=(
            jax.ShapeDtypeStruct((count, width), bf),
            jax.ShapeDtypeStruct((rows, width), f32),
        ),
        in_specs=[hbm, hbm, hbm, vmem, pl.BlockSpec(memory_space=pltpu.SMEM), hbm],
        out_specs=(vmem, vmem),
        scratch_shapes=[
            pltpu.VMEM((3, count, width), bf),
            pltpu.VMEM((freqs, width), f32),
            pltpu.VMEM((count, width), bf),
            pltpu.VMEM((heads, 2, C * count, hd), bf),
            pltpu.VMEM((heads, count, hd), bf),
            pltpu.VMEM((heads, count, hd), bf),
            pltpu.VMEM((heads, count, hd), bf),
            pltpu.VMEM((2, width), f32),
            pltpu.VMEM((n, 8, hd), f32),
            pltpu.VMEM((n, rows, hd), f32),
            pltpu.VMEM((n, padded, hd), f32),
            pltpu.VMEM((padded, hd), f32),
            pltpu.VMEM((count, hd), f32),
            pltpu.VMEM((count, hd), f32),
            dma((5,)),
            dma((heads,)), dma((heads,)), dma((heads,)), dma((heads,)),
            dma, dma, dma, dma, dma, dma,
        ],
        compiler_params=pltpu.CompilerParams(
            collective_id=0, has_side_effects=True, vmem_limit_bytes=VMEM_LIMIT if C <= 2 else 60 << 20
        ),
    )(
        pin(jnp.moveaxis(qkv[0, 0], 1, 0)),
        pin(qk_gain[0]),
        pin(mod_weight[0]),
        pin(positions),
        timesteps,
        pin(cotangent[0, 0]),
    )
    return attn_out[None, None], grad[None]


def solution(mesh):
    sizes = mesh.shape
    return jax.shard_map(
        functools.partial(local, sizes["segment"], sizes["ctx"], sizes["dp"]),
        mesh=mesh,
        in_specs=(
            P("segment", "dp", "ctx", None, None),
            P("segment", None, None),
            P("segment", None, None),
            P("dp", "ctx"),
            P("segment", "dp"),
            P("segment", "dp", "ctx", None),
        ),
        out_specs=(P("segment", "dp", "ctx", None), P("segment", ("ctx", "dp"), None)),
        check_vma=False,
    )
```

```python
import functools
import math

import jax
import jax.numpy as jnp
from jax import lax
from jax.experimental import pallas as pl
from jax.experimental.pallas import tpu as pltpu
from jax.sharding import PartitionSpec as P

HEAD_DIM = 128
GRID_ROWS = 45
GRID_COLS = 80
MESH = pl.DeviceIdType.MESH
LEAD = 8
LAG = 4
DIRECT = 4
FORWARD_AT = 6
VMEM_LIMIT = 24 << 20


def sincos(angle):
    turns = jnp.floor(angle * (2.0 / math.pi) + 0.5)
    quad = turns.astype(jnp.int32)
    r = angle - turns * 1.5703125
    r = r - turns * 4.837512969970703125e-4
    r = r - turns * 7.549789948768648e-8
    z = r * r
    sine = r + r * z * (-1.6666654611e-1 + z * (8.3321608736e-3 - z * 1.9515295891e-4))
    cosine = 1.0 - 0.5 * z + z * z * (
        4.166664568298827e-2 + z * (-1.388731625493765e-3 + z * 2.443315711809948e-5)
    )
    swap = (quad & 1) == 1
    s = jnp.where(swap, cosine, sine)
    c = jnp.where(swap, sine, cosine)
    s = jnp.where((quad & 2) == 2, -s, s)
    c = jnp.where(((quad + 1) & 2) == 2, -c, c)
    return s, c


def rope_angles(pos):
    count, hd = pos.shape
    half = hd // 2
    side = hd // 6
    first = half - 2 * side
    pair = lax.broadcasted_iota(jnp.int32, (8, hd), 1) % half
    group = jnp.where(pair < first, 0, jnp.where(pair < first + side, 1, 2))
    offset = jnp.where(group == 0, 0, jnp.where(group == 1, first, first + side))
    pairs_in = jnp.where(group == 0, first, side).astype(jnp.float32)
    freq = jnp.exp((pair - offset).astype(jnp.float32) / pairs_in * -math.log(10000.0))[0:1]
    group = group[0:1]
    frame = (pos // (GRID_ROWS * GRID_COLS)).astype(jnp.float32)
    row = (pos // GRID_COLS % GRID_ROWS).astype(jnp.float32)
    col = (pos % GRID_COLS).astype(jnp.float32)
    return jnp.where(group == 0, frame, jnp.where(group == 1, row, col)) * freq


def body(
    S, C, D, heads, freqs,
    x_ref, gain_ref, w_ref, pos_ref, t_ref, cot_ref,
    out_ref, grad_ref,
    xv, wv, cotv, kv, qbuf, abuf, rbuf, direct, gains, tbuf, ebuf, cbuf, gate, cosv, sinv,
    load_sem, kv_send, kv_recv, a_send, a_recv, g_send, g_recv, t_send, t_recv, c_send, c_recv,
    b_send, b_recv, bx_send, bx_recv,
):
    n = C * D
    count = x_ref.shape[1]
    rows = freqs // n
    hd = HEAD_DIM
    early = heads - direct.shape[0]
    seg = lax.axis_index("segment")
    ctx = lax.axis_index("ctx")
    dp = lax.axis_index("dp")
    me = ctx * D + dp
    after = {"segment": lax.rem(seg + 1, S)}
    before = {"segment": lax.rem(seg + S - 1, S)}
    peers = []
    for r in range(1, n):
        p = lax.rem(me + r, n)
        peers.append({"ctx": p // D, "dp": lax.rem(p, D)})
    ring = [{"ctx": lax.rem(ctx + r, C)} for r in range(1, C)]

    def cols(h):
        return pl.ds(pl.multiple_of(h * hd, hd), hd)

    loads = [
        pltpu.make_async_copy(x_ref.at[1], xv.at[1], load_sem.at[1]),
        pltpu.make_async_copy(x_ref.at[0], xv.at[0], load_sem.at[0]),
        pltpu.make_async_copy(x_ref.at[2], xv.at[2], load_sem.at[2]),
        pltpu.make_async_copy(w_ref, wv, load_sem.at[3]),
        pltpu.make_async_copy(cot_ref, cotv, load_sem.at[4]),
    ]
    for load in loads:
        load.start()
    step = t_ref[0, 0].astype(jnp.float32)
    tbuf[0] = jnp.full((8, hd), step, jnp.float32)

    barrier = pltpu.get_barrier_semaphore()
    for who in peers + [after, before]:
        pl.semaphore_signal(barrier, inc=1, device_id=who, device_id_type=MESH)
    pl.semaphore_wait(barrier, n + 1)

    gain_copy = pltpu.make_async_remote_copy(
        src_ref=gain_ref, dst_ref=gains, send_sem=g_send, recv_sem=g_recv,
        device_id=before, device_id_type=MESH,
    )
    gain_copy.start()

    def send_values(h):
        for r in range(1, C):
            pltpu.make_async_remote_copy(
                src_ref=x_ref.at[2, :, cols(h)],
                dst_ref=kv.at[h, 1, pl.ds(r * count, count), :],
                send_sem=kv_send.at[h], recv_sem=kv_recv.at[h],
                device_id=ring[r - 1], device_id_type=MESH,
            ).start()

    def send_keys(h):
        for r in range(1, C):
            pltpu.make_async_remote_copy(
                src_ref=kv.at[h, 0, pl.ds(0, count), :],
                dst_ref=kv.at[h, 0, pl.ds(r * count, count), :],
                send_sem=kv_send.at[h], recv_sem=kv_recv.at[h],
                device_id=ring[r - 1], device_id_type=MESH,
            ).start()

    lead = min(LEAD, early)

    @pl.loop(0, lead)
    def _(h):
        send_values(h)

    for r in range(1, n):
        pltpu.make_async_remote_copy(
            src_ref=tbuf.at[0], dst_ref=tbuf.at[r], send_sem=t_send, recv_sem=t_recv,
            device_id=peers[r - 1], device_id_type=MESH,
        ).start()

    pos = jnp.transpose(jnp.broadcast_to(pos_ref[...], (hd, count)))
    s, c = sincos(rope_angles(pos))
    lane = lax.broadcasted_iota(jnp.int32, (count, hd), 1)
    cosv[...] = c
    sinv[...] = jnp.where(lane < hd // 2, -s, s)

    def inverse_norm(which):
        def add(h, acc):
            x = xv[which, :, cols(h)].astype(jnp.float32)
            return acc + x * x

        total = lax.fori_loop(0, heads, add, jnp.zeros((count, hd), jnp.float32))
        mean = jnp.sum(total, axis=1, keepdims=True) / (heads * hd)
        return lax.rsqrt(mean + 1e-06)

    def turned(which, h, inv):
        x = xv[which, :, cols(h)].astype(jnp.float32)
        x = x * inv * gains[which : which + 1, cols(h)]
        return (x * cosv[...] + pltpu.roll(x, hd // 2, 1) * sinv[...]).astype(jnp.bfloat16)

    loads[0].wait()
    inv_k = inverse_norm(1)
    loads[1].wait()
    inv_q = inverse_norm(0)
    gain_copy.wait_recv()

    def hand_over(source, part, b):
        pltpu.make_async_remote_copy(
            src_ref=source, dst_ref=direct.at[b, part, pl.ds(0, count), :],
            send_sem=b_send.at[b], recv_sem=b_recv.at[b], device_id=after, device_id_type=MESH,
        ).start()

    def forward(b):
        here = direct.at[b, :, pl.ds(0, count), :]
        pltpu.make_async_copy(here, here, b_recv.at[b]).wait()
        for r in range(1, C):
            pltpu.make_async_remote_copy(
                src_ref=direct.at[b, pl.ds(0, 2), pl.ds(0, count), :],
                dst_ref=direct.at[b, pl.ds(0, 2), pl.ds(r * count, count), :],
                send_sem=bx_send.at[b], recv_sem=bx_recv.at[b],
                device_id=ring[r - 1], device_id_type=MESH,
            ).start()

    @pl.loop(early, heads)
    def _(h):
        kv[h, 0, 0:count, :] = turned(1, h, inv_k)
        qbuf[h] = turned(0, h, inv_q)
        hand_over(x_ref.at[2, :, cols(h)], 1, h - early)
        hand_over(kv.at[h, 0, pl.ds(0, count), :], 0, h - early)
        hand_over(qbuf.at[h], 2, h - early)

    @pl.loop(0, early)
    def _(h):
        kv[h, 0, 0:count, :] = turned(1, h, inv_k)
        send_keys(h)

        @pl.when(h + lead < early)
        def _():
            send_values(h + lead)

    loads[2].wait()

    @pl.loop(0, early)
    def _(h):
        qbuf[h] = turned(0, h, inv_q)
        kv[h, 1, 0:count, :] = xv[2, :, cols(h)]

    half = freqs // 2
    decay = -math.log(10000.0) / half
    index = lax.broadcasted_iota(jnp.int32, (half, hd), 0).astype(jnp.float32)
    es, ec = sincos(step * jnp.exp(index * decay))
    loads[3].wait()

    @pl.loop(0, heads)
    def _(h):
        part = wv[0:half, cols(h)] * ec + wv[half:freqs, cols(h)] * es
        gate[pl.ds(h, 1), :] = jnp.sum(part, axis=0, keepdims=True)

    if n > 1:
        pltpu.make_async_copy(tbuf.at[pl.ds(1, n - 1)], tbuf.at[pl.ds(1, n - 1)], t_recv).wait()
    at = lax.broadcasted_iota(jnp.int32, (rows, hd), 0) + me * rows
    freq = jnp.exp((at % half).astype(jnp.float32) * decay)
    for j in range(n):
        s, c = sincos(tbuf[j, 0:1, :] * freq)
        ebuf[j] = jnp.where(at < half, c, s)
    loads[4].wait()

    scale = 1.0 / hd**0.5

    def mix(queries, keys, values):
        scores = lax.dot_general(
            queries, keys, (((1,), (1,)), ((), ())), preferred_element_type=jnp.float32
        ) * scale
        expo = jnp.exp(scores - jnp.max(scores, axis=1, keepdims=True))
        total = jnp.sum(expo, axis=1, keepdims=True)
        mixed = jnp.dot(expo.astype(jnp.bfloat16), values, preferred_element_type=jnp.float32)
        return mixed / total

    def attend(h):
        arrived = kv.at[h, :, pl.ds(count, (C - 1) * count), :]
        pltpu.make_async_copy(arrived, arrived, kv_recv.at[h]).wait()
        abuf[h] = mix(qbuf[h], kv[h, 0], kv[h, 1]).astype(jnp.bfloat16)
        pltpu.make_async_remote_copy(
            src_ref=abuf.at[h], dst_ref=rbuf.at[h], send_sem=a_send.at[h], recv_sem=a_recv.at[h],
            device_id=after, device_id_type=MESH,
        ).start()

    def use(h, attn):
        out_ref[:, cols(h)] = (attn * gate[pl.ds(h, 1), :]).astype(jnp.bfloat16)
        cot = cotv[:, cols(h)].astype(jnp.float32)
        cbuf[0, pl.ds(h, 1), :] = jnp.sum(attn * cot, axis=0, keepdims=True)

    def finish(h):
        pltpu.make_async_copy(rbuf.at[h], rbuf.at[h], a_recv.at[h]).wait()
        use(h, rbuf[h].astype(jnp.float32))

    @pl.loop(0, early)
    def _(h):
        attend(h)

        @pl.when(h == min(FORWARD_AT, early - 1))
        def _():
            @pl.loop(0, heads - early)
            def _(b):
                forward(b)

        @pl.when(h >= LAG)
        def _():
            finish(h - LAG)

    @pl.loop(max(early - LAG, 0), early)
    def _(h):
        finish(h)

    @pl.loop(early, heads)
    def _(h):
        b = h - early
        arrived = direct.at[b, pl.ds(0, 2), pl.ds(count, (C - 1) * count), :]
        pltpu.make_async_copy(arrived, arrived, bx_recv.at[b]).wait()
        use(h, mix(direct[b, 2, 0:count, :], direct[b, 0], direct[b, 1]))

    for r in range(1, n):
        pltpu.make_async_remote_copy(
            src_ref=cbuf.at[0], dst_ref=cbuf.at[r], send_sem=c_send, recv_sem=c_recv,
            device_id=peers[r - 1], device_id_type=MESH,
        ).start()
    pltpu.make_async_copy(cbuf.at[pl.ds(1, n - 1)], cbuf.at[pl.ds(1, n - 1)], c_recv).wait()

    @pl.loop(0, heads)
    def _(h):
        acc = ebuf[0] * cbuf[0, pl.ds(h, 1), :]
        for j in range(1, n):
            acc = acc + ebuf[j] * cbuf[j, pl.ds(h, 1), :]
        grad_ref[:, cols(h)] = acc

    gain_copy.wait_send()
    pltpu.make_async_copy(tbuf.at[pl.ds(1, n - 1)], tbuf.at[pl.ds(1, n - 1)], t_send).wait()
    pltpu.make_async_copy(cbuf.at[pl.ds(1, n - 1)], cbuf.at[pl.ds(1, n - 1)], c_send).wait()

    @pl.loop(0, heads - early)
    def _(b):
        handed = direct.at[b, :, pl.ds(0, count), :]
        pltpu.make_async_copy(handed, handed, b_send.at[b]).wait()
        sent = direct.at[b, pl.ds(0, 2), pl.ds(count, (C - 1) * count), :]
        pltpu.make_async_copy(sent, sent, bx_send.at[b]).wait()

    @pl.loop(0, early)
    def _(h):
        sent = kv.at[h, :, pl.ds(count, (C - 1) * count), :]
        pltpu.make_async_copy(sent, sent, kv_send.at[h]).wait()
        pltpu.make_async_copy(abuf.at[h], abuf.at[h], a_send.at[h]).wait()


def local(S, C, D, qkv, qk_gain, mod_weight, positions, timesteps, cotangent):
    count, _, width = qkv.shape[2:]
    freqs = mod_weight.shape[1]
    heads = width // HEAD_DIM
    n = C * D
    rows = freqs // n
    hd = HEAD_DIM
    last = min(DIRECT, heads - 1)
    padded = -(-heads // 8) * 8
    bf, f32 = jnp.bfloat16, jnp.float32
    vmem = pl.BlockSpec(memory_space=pltpu.VMEM)
    hbm = pl.BlockSpec(memory_space=pltpu.HBM)
    dma = pltpu.SemaphoreType.DMA
    pin = functools.partial(pltpu.with_memory_space_constraint, memory_space=pltpu.HBM)
    attn_out, grad = pl.pallas_call(
        functools.partial(body, S, C, D, heads, freqs),
        out_shape=(
            jax.ShapeDtypeStruct((count, width), bf),
            jax.ShapeDtypeStruct((rows, width), f32),
        ),
        in_specs=[hbm, hbm, hbm, vmem, pl.BlockSpec(memory_space=pltpu.SMEM), hbm],
        out_specs=(vmem, vmem),
        scratch_shapes=[
            pltpu.VMEM((3, count, width), bf),
            pltpu.VMEM((freqs, width), f32),
            pltpu.VMEM((count, width), bf),
            pltpu.VMEM((heads, 2, C * count, hd), bf),
            pltpu.VMEM((heads, count, hd), bf),
            pltpu.VMEM((heads, count, hd), bf),
            pltpu.VMEM((heads, count, hd), bf),
            pltpu.VMEM((last, 3, C * count, hd), bf),
            pltpu.VMEM((2, width), f32),
            pltpu.VMEM((n, 8, hd), f32),
            pltpu.VMEM((n, rows, hd), f32),
            pltpu.VMEM((n, padded, hd), f32),
            pltpu.VMEM((padded, hd), f32),
            pltpu.VMEM((count, hd), f32),
            pltpu.VMEM((count, hd), f32),
            dma((5,)),
            dma((heads,)), dma((heads,)), dma((heads,)), dma((heads,)),
            dma, dma, dma, dma, dma, dma,
            dma((last,)), dma((last,)), dma((last,)), dma((last,)),
        ],
        compiler_params=pltpu.CompilerParams(
            collective_id=0, has_side_effects=True, vmem_limit_bytes=VMEM_LIMIT if C <= 2 else 60 << 20
        ),
    )(
        pin(jnp.moveaxis(qkv[0, 0], 1, 0)),
        pin(qk_gain[0]),
        pin(mod_weight[0]),
        pin(positions),
        timesteps,
        pin(cotangent[0, 0]),
    )
    return attn_out[None, None], grad[None]


def solution(mesh):
    sizes = mesh.shape
    return jax.shard_map(
        functools.partial(local, sizes["segment"], sizes["ctx"], sizes["dp"]),
        mesh=mesh,
        in_specs=(
            P("segment", "dp", "ctx", None, None),
            P("segment", None, None),
            P("segment", None, None),
            P("dp", "ctx"),
            P("segment", "dp"),
            P("segment", "dp", "ctx", None),
        ),
        out_specs=(P("segment", "dp", "ctx", None), P("segment", ("ctx", "dp"), None)),
        check_vma=False,
    )
```

```python
import functools
import math

import jax
import jax.numpy as jnp
from jax import lax
from jax.experimental import pallas as pl
from jax.experimental.pallas import tpu as pltpu
from jax.sharding import PartitionSpec as P

HEAD_DIM = 128
GRID_ROWS = 45
GRID_COLS = 80
MESH = pl.DeviceIdType.MESH
LEAD = 8
LAG = 4
DIRECT = 4
FORWARD_AT = 6
VMEM_LIMIT = 24 << 20


def sincos(angle):
    turns = jnp.floor(angle * (2.0 / math.pi) + 0.5)
    quad = turns.astype(jnp.int32)
    r = angle - turns * 1.5703125
    r = r - turns * 4.837512969970703125e-4
    r = r - turns * 7.549789948768648e-8
    z = r * r
    sine = r + r * z * (-1.6666654611e-1 + z * (8.3321608736e-3 - z * 1.9515295891e-4))
    cosine = 1.0 - 0.5 * z + z * z * (
        4.166664568298827e-2 + z * (-1.388731625493765e-3 + z * 2.443315711809948e-5)
    )
    swap = (quad & 1) == 1
    s = jnp.where(swap, cosine, sine)
    c = jnp.where(swap, sine, cosine)
    s = jnp.where((quad & 2) == 2, -s, s)
    c = jnp.where(((quad + 1) & 2) == 2, -c, c)
    return s, c


def rope_angles(pos):
    count, hd = pos.shape
    half = hd // 2
    side = hd // 6
    first = half - 2 * side
    pair = lax.broadcasted_iota(jnp.int32, (8, hd), 1) % half
    group = jnp.where(pair < first, 0, jnp.where(pair < first + side, 1, 2))
    offset = jnp.where(group == 0, 0, jnp.where(group == 1, first, first + side))
    pairs_in = jnp.where(group == 0, first, side).astype(jnp.float32)
    freq = jnp.exp((pair - offset).astype(jnp.float32) / pairs_in * -math.log(10000.0))[0:1]
    group = group[0:1]
    frame = (pos // (GRID_ROWS * GRID_COLS)).astype(jnp.float32)
    row = (pos // GRID_COLS % GRID_ROWS).astype(jnp.float32)
    col = (pos % GRID_COLS).astype(jnp.float32)
    return jnp.where(group == 0, frame, jnp.where(group == 1, row, col)) * freq


def body(
    S, C, D, heads, freqs,
    x_ref, gain_ref, w_ref, pos_ref, t_ref, cot_ref,
    out_ref, cbuf, ebuf,
    xv, wv, cotv, kv, qbuf, abuf, rbuf, direct, gains, tbuf, gate, cosv, sinv,
    load_sem, kv_send, kv_recv, a_send, a_recv, g_send, g_recv, t_send, t_recv, c_send, c_recv,
    b_send, b_recv, bx_send, bx_recv, down_sem, up_sem,
):
    n = C * D
    count = x_ref.shape[1]
    rows = freqs // n
    hd = HEAD_DIM
    early = heads - direct.shape[0]
    seg = lax.axis_index("segment")
    ctx = lax.axis_index("ctx")
    dp = lax.axis_index("dp")
    me = ctx * D + dp
    after = {"segment": lax.rem(seg + 1, S)}
    before = {"segment": lax.rem(seg + S - 1, S)}
    peers = []
    for r in range(1, n):
        p = lax.rem(me + r, n)
        peers.append({"ctx": p // D, "dp": lax.rem(p, D)})
    ring = [{"ctx": lax.rem(ctx + r, C)} for r in range(1, C)]

    def cols(h):
        return pl.ds(pl.multiple_of(h * hd, hd), hd)

    loads = [
        pltpu.make_async_copy(x_ref.at[1], xv.at[1], load_sem.at[1]),
        pltpu.make_async_copy(x_ref.at[0], xv.at[0], load_sem.at[0]),
        pltpu.make_async_copy(x_ref.at[2], xv.at[2], load_sem.at[2]),
        pltpu.make_async_copy(w_ref, wv, load_sem.at[3]),
        pltpu.make_async_copy(cot_ref, cotv, load_sem.at[4]),
    ]
    for load in loads:
        load.start()
    step = t_ref[0, 0].astype(jnp.float32)
    tbuf[0] = jnp.full((8, hd), step, jnp.float32)

    barrier = pltpu.get_barrier_semaphore()
    def greet(who):
        pl.semaphore_signal(barrier, inc=1, device_id=who, device_id_type=MESH)

    for who in peers:
        greet(who)
    chain = S > 2
    if chain:
        @pl.when(seg < S - 1)
        def _():
            greet(after)

        @pl.when(seg > 0)
        def _():
            greet(before)

        ends = jnp.where(seg == 0, 1, 0) + jnp.where(seg == S - 1, 1, 0)
        pl.semaphore_wait(barrier, n + 1 - ends)
    else:
        greet(after)
        greet(before)
        pl.semaphore_wait(barrier, n + 1)

    gain_copy = pltpu.make_async_remote_copy(
        src_ref=gain_ref, dst_ref=gains, send_sem=g_send, recv_sem=g_recv,
        device_id=before, device_id_type=MESH,
    )

    def send_values(h):
        for r in range(1, C):
            pltpu.make_async_remote_copy(
                src_ref=x_ref.at[2, :, cols(h)],
                dst_ref=kv.at[h, 1, pl.ds(r * count, count), :],
                send_sem=kv_send.at[h], recv_sem=kv_recv.at[h],
                device_id=ring[r - 1], device_id_type=MESH,
            ).start()

    def send_keys(h):
        for r in range(1, C):
            pltpu.make_async_remote_copy(
                src_ref=kv.at[h, 0, pl.ds(0, count), :],
                dst_ref=kv.at[h, 0, pl.ds(r * count, count), :],
                send_sem=kv_send.at[h], recv_sem=kv_recv.at[h],
                device_id=ring[r - 1], device_id_type=MESH,
            ).start()

    lead = min(LEAD, early)

    @pl.loop(0, lead)
    def _(h):
        send_values(h)

    for r in range(1, n):
        pltpu.make_async_remote_copy(
            src_ref=tbuf.at[0], dst_ref=tbuf.at[r], send_sem=t_send, recv_sem=t_recv,
            device_id=peers[r - 1], device_id_type=MESH,
        ).start()

    def tell(sem, who):
        pl.semaphore_signal(sem, inc=1, device_id=who, device_id_type=MESH)

    if chain:
        @pl.when(seg > 0)
        def _():
            gain_copy.start()

        @pl.when(seg == S - 2)
        def _():
            tell(down_sem, before)

        @pl.when(seg == 1)
        def _():
            tell(up_sem, after)

        @pl.when(seg < S - 2)
        def _():
            pl.semaphore_wait(down_sem, 1)

            @pl.when(seg > 0)
            def _():
                tell(down_sem, before)

        @pl.when(seg == 0)
        def _():
            gain_copy.start()

        @pl.when(seg > 1)
        def _():
            pl.semaphore_wait(up_sem, 1)

            @pl.when(seg < S - 1)
            def _():
                tell(up_sem, after)
    else:
        gain_copy.start()

    pos = jnp.transpose(jnp.broadcast_to(pos_ref[...], (hd, count)))
    s, c = sincos(rope_angles(pos))
    lane = lax.broadcasted_iota(jnp.int32, (count, hd), 1)
    cosv[...] = c
    sinv[...] = jnp.where(lane < hd // 2, -s, s)

    def inverse_norm(which):
        def add(h, acc):
            x = xv[which, :, cols(h)].astype(jnp.float32)
            return acc + x * x

        total = lax.fori_loop(0, heads, add, jnp.zeros((count, hd), jnp.float32))
        mean = jnp.sum(total, axis=1, keepdims=True) / (heads * hd)
        return lax.rsqrt(mean + 1e-06)

    def turned(which, h, inv):
        x = xv[which, :, cols(h)].astype(jnp.float32)
        x = x * inv * gains[which : which + 1, cols(h)]
        return (x * cosv[...] + pltpu.roll(x, hd // 2, 1) * sinv[...]).astype(jnp.bfloat16)

    loads[0].wait()
    inv_k = inverse_norm(1)
    loads[1].wait()
    inv_q = inverse_norm(0)
    gain_copy.wait_recv()

    def hand_over(source, part, b):
        pltpu.make_async_remote_copy(
            src_ref=source, dst_ref=direct.at[b, part, pl.ds(0, count), :],
            send_sem=b_send.at[b], recv_sem=b_recv.at[b], device_id=after, device_id_type=MESH,
        ).start()

    def forward(b):
        here = direct.at[b, :, pl.ds(0, count), :]
        pltpu.make_async_copy(here, here, b_recv.at[b]).wait()
        for r in range(1, C):
            pltpu.make_async_remote_copy(
                src_ref=direct.at[b, pl.ds(0, 2), pl.ds(0, count), :],
                dst_ref=direct.at[b, pl.ds(0, 2), pl.ds(r * count, count), :],
                send_sem=bx_send.at[b], recv_sem=bx_recv.at[b],
                device_id=ring[r - 1], device_id_type=MESH,
            ).start()

    @pl.loop(early, heads)
    def _(h):
        kv[h, 0, 0:count, :] = turned(1, h, inv_k)
        qbuf[h] = turned(0, h, inv_q)
        hand_over(x_ref.at[2, :, cols(h)], 1, h - early)
        hand_over(kv.at[h, 0, pl.ds(0, count), :], 0, h - early)
        hand_over(qbuf.at[h], 2, h - early)

    @pl.loop(0, early)
    def _(h):
        kv[h, 0, 0:count, :] = turned(1, h, inv_k)
        send_keys(h)

        @pl.when(h + lead < early)
        def _():
            send_values(h + lead)

    loads[2].wait()

    @pl.loop(0, early)
    def _(h):
        qbuf[h] = turned(0, h, inv_q)
        kv[h, 1, 0:count, :] = xv[2, :, cols(h)]

    half = freqs // 2
    decay = -math.log(10000.0) / half
    index = lax.broadcasted_iota(jnp.int32, (half, hd), 0).astype(jnp.float32)
    es, ec = sincos(step * jnp.exp(index * decay))
    loads[3].wait()

    @pl.loop(0, heads)
    def _(h):
        part = wv[0:half, cols(h)] * ec + wv[half:freqs, cols(h)] * es
        gate[pl.ds(h, 1), :] = jnp.sum(part, axis=0, keepdims=True)

    if n > 1:
        pltpu.make_async_copy(tbuf.at[pl.ds(1, n - 1)], tbuf.at[pl.ds(1, n - 1)], t_recv).wait()
    at = lax.broadcasted_iota(jnp.int32, (rows, hd), 0) + me * rows
    freq = jnp.exp((at % half).astype(jnp.float32) * decay)
    for j in range(n):
        s, c = sincos(tbuf[j, 0:1, :] * freq)
        ebuf[j] = jnp.where(at < half, c, s)
    loads[4].wait()

    scale = 1.0 / hd**0.5

    def mix(queries, keys, values):
        scores = lax.dot_general(
            queries, keys, (((1,), (1,)), ((), ())), preferred_element_type=jnp.float32
        ) * scale
        expo = jnp.exp(scores - jnp.max(scores, axis=1, keepdims=True))
        total = jnp.sum(expo, axis=1, keepdims=True)
        mixed = jnp.dot(expo.astype(jnp.bfloat16), values, preferred_element_type=jnp.float32)
        return mixed / total

    def attend(h):
        arrived = kv.at[h, :, pl.ds(count, (C - 1) * count), :]
        pltpu.make_async_copy(arrived, arrived, kv_recv.at[h]).wait()
        abuf[h] = mix(qbuf[h], kv[h, 0], kv[h, 1]).astype(jnp.bfloat16)
        pltpu.make_async_remote_copy(
            src_ref=abuf.at[h], dst_ref=rbuf.at[h], send_sem=a_send.at[h], recv_sem=a_recv.at[h],
            device_id=after, device_id_type=MESH,
        ).start()

    def use(h, attn):
        out_ref[:, cols(h)] = (attn * gate[pl.ds(h, 1), :]).astype(jnp.bfloat16)
        cot = cotv[:, cols(h)].astype(jnp.float32)
        cbuf[0, pl.ds(h, 1), :] = jnp.sum(attn * cot, axis=0, keepdims=True)

    def finish(h):
        pltpu.make_async_copy(rbuf.at[h], rbuf.at[h], a_recv.at[h]).wait()
        use(h, rbuf[h].astype(jnp.float32))

    @pl.loop(0, early)
    def _(h):
        attend(h)

        @pl.when(h == min(FORWARD_AT, early - 1))
        def _():
            @pl.loop(0, heads - early)
            def _(b):
                forward(b)

        @pl.when(h >= LAG)
        def _():
            finish(h - LAG)

    @pl.loop(max(early - LAG, 0), early)
    def _(h):
        finish(h)

    @pl.loop(early, heads)
    def _(h):
        b = h - early
        arrived = direct.at[b, pl.ds(0, 2), pl.ds(count, (C - 1) * count), :]
        pltpu.make_async_copy(arrived, arrived, bx_recv.at[b]).wait()
        use(h, mix(direct[b, 2, 0:count, :], direct[b, 0], direct[b, 1]))

    for r in range(1, n):
        pltpu.make_async_remote_copy(
            src_ref=cbuf.at[0], dst_ref=cbuf.at[r], send_sem=c_send, recv_sem=c_recv,
            device_id=peers[r - 1], device_id_type=MESH,
        ).start()
    pltpu.make_async_copy(cbuf.at[pl.ds(1, n - 1)], cbuf.at[pl.ds(1, n - 1)], c_recv).wait()

    gain_copy.wait_send()
    pltpu.make_async_copy(tbuf.at[pl.ds(1, n - 1)], tbuf.at[pl.ds(1, n - 1)], t_send).wait()
    pltpu.make_async_copy(cbuf.at[pl.ds(1, n - 1)], cbuf.at[pl.ds(1, n - 1)], c_send).wait()

    @pl.loop(0, heads - early)
    def _(b):
        handed = direct.at[b, :, pl.ds(0, count), :]
        pltpu.make_async_copy(handed, handed, b_send.at[b]).wait()
        sent = direct.at[b, pl.ds(0, 2), pl.ds(count, (C - 1) * count), :]
        pltpu.make_async_copy(sent, sent, bx_send.at[b]).wait()

    @pl.loop(0, early)
    def _(h):
        sent = kv.at[h, :, pl.ds(count, (C - 1) * count), :]
        pltpu.make_async_copy(sent, sent, kv_send.at[h]).wait()
        pltpu.make_async_copy(abuf.at[h], abuf.at[h], a_send.at[h]).wait()


def store(n, heads, attn_ref, chan_ref, emb_ref, out_ref, grad_ref, total, out_sem, grad_sem):
    copy = pltpu.make_async_copy(attn_ref, out_ref, out_sem)
    copy.start()
    hd = HEAD_DIM
    for h in range(heads):
        acc = emb_ref[0] * chan_ref[0, h : h + 1, :]
        for j in range(1, n):
            acc = acc + emb_ref[j] * chan_ref[j, h : h + 1, :]
        total[h] = acc
        pltpu.make_async_copy(total.at[h], grad_ref.at[:, h * hd : (h + 1) * hd], grad_sem.at[h]).start()
    for h in range(heads):
        pltpu.make_async_copy(total.at[h], grad_ref.at[:, h * hd : (h + 1) * hd], grad_sem.at[h]).wait()
    copy.wait()


def local(S, C, D, qkv, qk_gain, mod_weight, positions, timesteps, cotangent):
    count, _, width = qkv.shape[2:]
    freqs = mod_weight.shape[1]
    heads = width // HEAD_DIM
    n = C * D
    rows = freqs // n
    hd = HEAD_DIM
    last = min(DIRECT, heads - 1)
    padded = -(-heads // 8) * 8
    bf, f32 = jnp.bfloat16, jnp.float32
    vmem = pl.BlockSpec(memory_space=pltpu.VMEM)
    hbm = pl.BlockSpec(memory_space=pltpu.HBM)
    dma = pltpu.SemaphoreType.DMA
    pin = functools.partial(pltpu.with_memory_space_constraint, memory_space=pltpu.HBM)
    attn, chans, embs = pl.pallas_call(
        functools.partial(body, S, C, D, heads, freqs),
        out_shape=(
            jax.ShapeDtypeStruct((count, width), bf),
            jax.ShapeDtypeStruct((n, padded, hd), f32),
            jax.ShapeDtypeStruct((n, rows, hd), f32),
        ),
        in_specs=[hbm, hbm, hbm, vmem, pl.BlockSpec(memory_space=pltpu.SMEM), hbm],
        out_specs=(vmem, vmem, vmem),
        scratch_shapes=[
            pltpu.VMEM((3, count, width), bf),
            pltpu.VMEM((freqs, width), f32),
            pltpu.VMEM((count, width), bf),
            pltpu.VMEM((heads, 2, C * count, hd), bf),
            pltpu.VMEM((heads, count, hd), bf),
            pltpu.VMEM((heads, count, hd), bf),
            pltpu.VMEM((heads, count, hd), bf),
            pltpu.VMEM((last, 3, C * count, hd), bf),
            pltpu.VMEM((2, width), f32),
            pltpu.VMEM((n, 8, hd), f32),
            pltpu.VMEM((padded, hd), f32),
            pltpu.VMEM((count, hd), f32),
            pltpu.VMEM((count, hd), f32),
            dma((5,)),
            dma((heads,)), dma((heads,)), dma((heads,)), dma((heads,)),
            dma, dma, dma, dma, dma, dma,
            dma((last,)), dma((last,)), dma((last,)), dma((last,)),
            pltpu.SemaphoreType.REGULAR, pltpu.SemaphoreType.REGULAR,
        ],
        compiler_params=pltpu.CompilerParams(
            collective_id=0, has_side_effects=True, vmem_limit_bytes=VMEM_LIMIT if C <= 2 else 60 << 20
        ),
    )(
        pin(jnp.moveaxis(qkv[0, 0], 1, 0)),
        pin(qk_gain[0]),
        pin(mod_weight[0]),
        pin(positions),
        timesteps,
        pin(cotangent[0, 0]),
    )
    attn_out, grad = pl.pallas_call(
        functools.partial(store, n, heads),
        out_shape=(
            jax.ShapeDtypeStruct((count, width), bf),
            jax.ShapeDtypeStruct((rows, width), f32),
        ),
        in_specs=[pl.BlockSpec(memory_space=pl.ANY), vmem, vmem],
        out_specs=(pl.BlockSpec(memory_space=pl.ANY), pl.BlockSpec(memory_space=pl.ANY)),
        scratch_shapes=[pltpu.VMEM((heads, rows, hd), f32), dma, dma((heads,))],
        compiler_params=pltpu.CompilerParams(vmem_limit_bytes=4 << 20),
    )(attn, chans, embs)
    return attn_out[None, None], grad[None]


def solution(mesh):
    sizes = mesh.shape
    return jax.shard_map(
        functools.partial(local, sizes["segment"], sizes["ctx"], sizes["dp"]),
        mesh=mesh,
        in_specs=(
            P("segment", "dp", "ctx", None, None),
            P("segment", None, None),
            P("segment", None, None),
            P("dp", "ctx"),
            P("segment", "dp"),
            P("segment", "dp", "ctx", None),
        ),
        out_specs=(P("segment", "dp", "ctx", None), P("segment", ("ctx", "dp"), None)),
        check_vma=False,
    )
```

```python
import functools
import math

import jax
import jax.numpy as jnp
from jax import lax
from jax.experimental import pallas as pl
from jax.experimental.pallas import tpu as pltpu
from jax.sharding import PartitionSpec as P

HEAD_DIM = 128
GRID_ROWS = 45
GRID_COLS = 80
MESH = pl.DeviceIdType.MESH
LEAD = 8
LAG = 6
DIRECT = 5
FORWARD_AT = 6
VMEM_LIMIT = 24 << 20


def sincos(angle):
    turns = jnp.floor(angle * (2.0 / math.pi) + 0.5)
    quad = turns.astype(jnp.int32)
    r = angle - turns * 1.5703125
    r = r - turns * 4.837512969970703125e-4
    r = r - turns * 7.549789948768648e-8
    z = r * r
    sine = r + r * z * (-1.6666654611e-1 + z * (8.3321608736e-3 - z * 1.9515295891e-4))
    cosine = 1.0 - 0.5 * z + z * z * (
        4.166664568298827e-2 + z * (-1.388731625493765e-3 + z * 2.443315711809948e-5)
    )
    swap = (quad & 1) == 1
    s = jnp.where(swap, cosine, sine)
    c = jnp.where(swap, sine, cosine)
    s = jnp.where((quad & 2) == 2, -s, s)
    c = jnp.where(((quad + 1) & 2) == 2, -c, c)
    return s, c


def rope_angles(pos):
    count, hd = pos.shape
    half = hd // 2
    side = hd // 6
    first = half - 2 * side
    pair = lax.broadcasted_iota(jnp.int32, (8, hd), 1) % half
    group = jnp.where(pair < first, 0, jnp.where(pair < first + side, 1, 2))
    offset = jnp.where(group == 0, 0, jnp.where(group == 1, first, first + side))
    pairs_in = jnp.where(group == 0, first, side).astype(jnp.float32)
    freq = jnp.exp((pair - offset).astype(jnp.float32) / pairs_in * -math.log(10000.0))[0:1]
    group = group[0:1]
    frame = (pos // (GRID_ROWS * GRID_COLS)).astype(jnp.float32)
    row = (pos // GRID_COLS % GRID_ROWS).astype(jnp.float32)
    col = (pos % GRID_COLS).astype(jnp.float32)
    return jnp.where(group == 0, frame, jnp.where(group == 1, row, col)) * freq


def body(
    S, C, D, heads, freqs,
    x_ref, gain_ref, w_ref, pos_ref, t_ref, cot_ref,
    out_ref, cbuf, ebuf,
    xv, wv, cotv, kv, qbuf, abuf, rbuf, direct, gains, tbuf, gate, cosv, sinv,
    load_sem, kv_send, kv_recv, a_send, a_recv, g_send, g_recv, t_send, t_recv, c_send, c_recv,
    b_send, b_recv, bx_send, bx_recv, down_sem, up_sem,
):
    n = C * D
    count = x_ref.shape[1]
    rows = freqs // n
    hd = HEAD_DIM
    early = heads - direct.shape[0]
    seg = lax.axis_index("segment")
    ctx = lax.axis_index("ctx")
    dp = lax.axis_index("dp")
    me = ctx * D + dp
    after = {"segment": lax.rem(seg + 1, S)}
    before = {"segment": lax.rem(seg + S - 1, S)}
    peers = []
    for r in range(1, n):
        p = lax.rem(me + r, n)
        peers.append({"ctx": p // D, "dp": lax.rem(p, D)})
    ring = [{"ctx": lax.rem(ctx + r, C)} for r in range(1, C)]

    def cols(h):
        return pl.ds(pl.multiple_of(h * hd, hd), hd)

    loads = [
        pltpu.make_async_copy(x_ref.at[1], xv.at[1], load_sem.at[1]),
        pltpu.make_async_copy(x_ref.at[0], xv.at[0], load_sem.at[0]),
        pltpu.make_async_copy(x_ref.at[2], xv.at[2], load_sem.at[2]),
        pltpu.make_async_copy(w_ref, wv, load_sem.at[3]),
        pltpu.make_async_copy(cot_ref, cotv, load_sem.at[4]),
    ]
    for load in loads:
        load.start()
    step = t_ref[0, 0].astype(jnp.float32)
    tbuf[0] = jnp.full((8, hd), step, jnp.float32)

    barrier = pltpu.get_barrier_semaphore()
    def greet(who):
        pl.semaphore_signal(barrier, inc=1, device_id=who, device_id_type=MESH)

    for who in peers:
        greet(who)
    chain = S > 2
    if chain:
        @pl.when(seg < S - 1)
        def _():
            greet(after)

        @pl.when(seg > 0)
        def _():
            greet(before)

        ends = jnp.where(seg == 0, 1, 0) + jnp.where(seg == S - 1, 1, 0)
        pl.semaphore_wait(barrier, n + 1 - ends)
    else:
        greet(after)
        greet(before)
        pl.semaphore_wait(barrier, n + 1)

    gain_copy = pltpu.make_async_remote_copy(
        src_ref=gain_ref, dst_ref=gains, send_sem=g_send, recv_sem=g_recv,
        device_id=before, device_id_type=MESH,
    )

    def send_values(h):
        for r in range(1, C):
            pltpu.make_async_remote_copy(
                src_ref=x_ref.at[2, :, cols(h)],
                dst_ref=kv.at[h, 1, pl.ds(r * count, count), :],
                send_sem=kv_send.at[h], recv_sem=kv_recv.at[h],
                device_id=ring[r - 1], device_id_type=MESH,
            ).start()

    def send_keys(h):
        for r in range(1, C):
            pltpu.make_async_remote_copy(
                src_ref=kv.at[h, 0, pl.ds(0, count), :],
                dst_ref=kv.at[h, 0, pl.ds(r * count, count), :],
                send_sem=kv_send.at[h], recv_sem=kv_recv.at[h],
                device_id=ring[r - 1], device_id_type=MESH,
            ).start()

    lead = min(LEAD, early)

    @pl.loop(0, lead)
    def _(h):
        send_values(h)

    for r in range(1, n):
        pltpu.make_async_remote_copy(
            src_ref=tbuf.at[0], dst_ref=tbuf.at[r], send_sem=t_send, recv_sem=t_recv,
            device_id=peers[r - 1], device_id_type=MESH,
        ).start()

    def tell(sem, who):
        pl.semaphore_signal(sem, inc=1, device_id=who, device_id_type=MESH)

    if chain:
        @pl.when(seg > 0)
        def _():
            gain_copy.start()

        @pl.when(seg == S - 2)
        def _():
            tell(down_sem, before)

        @pl.when(seg == 1)
        def _():
            tell(up_sem, after)

        @pl.when(seg < S - 2)
        def _():
            pl.semaphore_wait(down_sem, 1)

            @pl.when(seg > 0)
            def _():
                tell(down_sem, before)

        @pl.when(seg == 0)
        def _():
            gain_copy.start()

        @pl.when(seg > 1)
        def _():
            pl.semaphore_wait(up_sem, 1)

            @pl.when(seg < S - 1)
            def _():
                tell(up_sem, after)
    else:
        gain_copy.start()

    pos = jnp.transpose(jnp.broadcast_to(pos_ref[...], (hd, count)))
    s, c = sincos(rope_angles(pos))
    lane = lax.broadcasted_iota(jnp.int32, (count, hd), 1)
    cosv[...] = c
    sinv[...] = jnp.where(lane < hd // 2, -s, s)

    def inverse_norm(which):
        def add(h, acc):
            x = xv[which, :, cols(h)].astype(jnp.float32)
            return acc + x * x

        total = lax.fori_loop(0, heads, add, jnp.zeros((count, hd), jnp.float32))
        mean = jnp.sum(total, axis=1, keepdims=True) / (heads * hd)
        return lax.rsqrt(mean + 1e-06)

    def turned(which, h, inv):
        x = xv[which, :, cols(h)].astype(jnp.float32)
        x = x * inv * gains[which : which + 1, cols(h)]
        return (x * cosv[...] + pltpu.roll(x, hd // 2, 1) * sinv[...]).astype(jnp.bfloat16)

    loads[0].wait()
    inv_k = inverse_norm(1)
    loads[1].wait()
    inv_q = inverse_norm(0)
    gain_copy.wait_recv()

    def hand_over(source, part, b):
        pltpu.make_async_remote_copy(
            src_ref=source, dst_ref=direct.at[b, part, pl.ds(0, count), :],
            send_sem=b_send.at[b], recv_sem=b_recv.at[b], device_id=after, device_id_type=MESH,
        ).start()

    def forward(b):
        here = direct.at[b, :, pl.ds(0, count), :]
        pltpu.make_async_copy(here, here, b_recv.at[b]).wait()
        for r in range(1, C):
            pltpu.make_async_remote_copy(
                src_ref=direct.at[b, pl.ds(0, 2), pl.ds(0, count), :],
                dst_ref=direct.at[b, pl.ds(0, 2), pl.ds(r * count, count), :],
                send_sem=bx_send.at[b], recv_sem=bx_recv.at[b],
                device_id=ring[r - 1], device_id_type=MESH,
            ).start()

    @pl.loop(early, heads)
    def _(h):
        kv[h, 0, 0:count, :] = turned(1, h, inv_k)
        qbuf[h] = turned(0, h, inv_q)
        hand_over(x_ref.at[2, :, cols(h)], 1, h - early)
        hand_over(kv.at[h, 0, pl.ds(0, count), :], 0, h - early)
        hand_over(qbuf.at[h], 2, h - early)

    @pl.loop(0, early)
    def _(h):
        kv[h, 0, 0:count, :] = turned(1, h, inv_k)
        send_keys(h)

        @pl.when(h + lead < early)
        def _():
            send_values(h + lead)

    loads[2].wait()

    @pl.loop(0, early)
    def _(h):
        qbuf[h] = turned(0, h, inv_q)
        kv[h, 1, 0:count, :] = xv[2, :, cols(h)]

    half = freqs // 2
    decay = -math.log(10000.0) / half
    index = lax.broadcasted_iota(jnp.int32, (half, hd), 0).astype(jnp.float32)
    es, ec = sincos(step * jnp.exp(index * decay))
    loads[3].wait()

    @pl.loop(0, heads)
    def _(h):
        part = wv[0:half, cols(h)] * ec + wv[half:freqs, cols(h)] * es
        gate[pl.ds(h, 1), :] = jnp.sum(part, axis=0, keepdims=True)

    if n > 1:
        pltpu.make_async_copy(tbuf.at[pl.ds(1, n - 1)], tbuf.at[pl.ds(1, n - 1)], t_recv).wait()
    at = lax.broadcasted_iota(jnp.int32, (rows, hd), 0) + me * rows
    freq = jnp.exp((at % half).astype(jnp.float32) * decay)
    for j in range(n):
        s, c = sincos(tbuf[j, 0:1, :] * freq)
        ebuf[j] = jnp.where(at < half, c, s)
    loads[4].wait()

    scale = 1.0 / hd**0.5

    def mix(queries, keys, values):
        scores = lax.dot_general(
            queries, keys, (((1,), (1,)), ((), ())), preferred_element_type=jnp.float32
        ) * scale
        expo = jnp.exp(scores - jnp.max(scores, axis=1, keepdims=True))
        total = jnp.sum(expo, axis=1, keepdims=True)
        mixed = jnp.dot(expo.astype(jnp.bfloat16), values, preferred_element_type=jnp.float32)
        return mixed / total

    def attend(h):
        arrived = kv.at[h, :, pl.ds(count, (C - 1) * count), :]
        pltpu.make_async_copy(arrived, arrived, kv_recv.at[h]).wait()
        abuf[h] = mix(qbuf[h], kv[h, 0], kv[h, 1]).astype(jnp.bfloat16)
        pltpu.make_async_remote_copy(
            src_ref=abuf.at[h], dst_ref=rbuf.at[h], send_sem=a_send.at[h], recv_sem=a_recv.at[h],
            device_id=after, device_id_type=MESH,
        ).start()

    def use(h, attn):
        out_ref[:, cols(h)] = (attn * gate[pl.ds(h, 1), :]).astype(jnp.bfloat16)
        cot = cotv[:, cols(h)].astype(jnp.float32)
        cbuf[0, pl.ds(h, 1), :] = jnp.sum(attn * cot, axis=0, keepdims=True)

    def finish(h):
        pltpu.make_async_copy(rbuf.at[h], rbuf.at[h], a_recv.at[h]).wait()
        use(h, rbuf[h].astype(jnp.float32))

    @pl.loop(0, early)
    def _(h):
        attend(h)

        @pl.when(h == min(FORWARD_AT, early - 1))
        def _():
            @pl.loop(0, heads - early)
            def _(b):
                forward(b)

        @pl.when(h >= LAG)
        def _():
            finish(h - LAG)

    @pl.loop(max(early - LAG, 0), early)
    def _(h):
        finish(h)

    split = early // 8 * 8

    def share_sums(low, high, part):
        for r in range(1, n):
            pltpu.make_async_remote_copy(
                src_ref=cbuf.at[0, pl.ds(low, high - low), :],
                dst_ref=cbuf.at[r, pl.ds(low, high - low), :],
                send_sem=c_send.at[part], recv_sem=c_recv.at[part],
                device_id=peers[r - 1], device_id_type=MESH,
            ).start()

    if split > 0:
        share_sums(0, split, 0)

    @pl.loop(early, heads)
    def _(h):
        b = h - early
        arrived = direct.at[b, pl.ds(0, 2), pl.ds(count, (C - 1) * count), :]
        pltpu.make_async_copy(arrived, arrived, bx_recv.at[b]).wait()
        use(h, mix(direct[b, 2, 0:count, :], direct[b, 0], direct[b, 1]))

    if n > 1:
        share_sums(split, cbuf.shape[1], 1)
        for part, (low, high) in enumerate(((0, split), (split, cbuf.shape[1]))):
            if high > low:
                others = cbuf.at[pl.ds(1, n - 1), pl.ds(low, high - low), :]
                pltpu.make_async_copy(others, others, c_recv.at[part]).wait()

    gain_copy.wait_send()
    pltpu.make_async_copy(tbuf.at[pl.ds(1, n - 1)], tbuf.at[pl.ds(1, n - 1)], t_send).wait()
    for part, (low, high) in enumerate(((0, split), (split, cbuf.shape[1]))):
        if n > 1 and high > low:
            others = cbuf.at[pl.ds(1, n - 1), pl.ds(low, high - low), :]
            pltpu.make_async_copy(others, others, c_send.at[part]).wait()

    @pl.loop(0, heads - early)
    def _(b):
        handed = direct.at[b, :, pl.ds(0, count), :]
        pltpu.make_async_copy(handed, handed, b_send.at[b]).wait()
        sent = direct.at[b, pl.ds(0, 2), pl.ds(count, (C - 1) * count), :]
        pltpu.make_async_copy(sent, sent, bx_send.at[b]).wait()

    @pl.loop(0, early)
    def _(h):
        sent = kv.at[h, :, pl.ds(count, (C - 1) * count), :]
        pltpu.make_async_copy(sent, sent, kv_send.at[h]).wait()
        pltpu.make_async_copy(abuf.at[h], abuf.at[h], a_send.at[h]).wait()


def store(n, heads, attn_ref, chan_ref, emb_ref, out_ref, grad_ref, total, out_sem, grad_sem):
    copy = pltpu.make_async_copy(attn_ref, out_ref, out_sem)
    copy.start()
    hd = HEAD_DIM
    for h in range(heads):
        acc = emb_ref[0] * chan_ref[0, h : h + 1, :]
        for j in range(1, n):
            acc = acc + emb_ref[j] * chan_ref[j, h : h + 1, :]
        total[h] = acc
        pltpu.make_async_copy(total.at[h], grad_ref.at[:, h * hd : (h + 1) * hd], grad_sem.at[h]).start()
    for h in range(heads):
        pltpu.make_async_copy(total.at[h], grad_ref.at[:, h * hd : (h + 1) * hd], grad_sem.at[h]).wait()
    copy.wait()


def local(S, C, D, qkv, qk_gain, mod_weight, positions, timesteps, cotangent):
    count, _, width = qkv.shape[2:]
    freqs = mod_weight.shape[1]
    heads = width // HEAD_DIM
    n = C * D
    rows = freqs // n
    hd = HEAD_DIM
    last = min(DIRECT, heads - 1)
    padded = -(-heads // 8) * 8
    bf, f32 = jnp.bfloat16, jnp.float32
    vmem = pl.BlockSpec(memory_space=pltpu.VMEM)
    hbm = pl.BlockSpec(memory_space=pltpu.HBM)
    dma = pltpu.SemaphoreType.DMA
    pin = functools.partial(pltpu.with_memory_space_constraint, memory_space=pltpu.HBM)
    attn, chans, embs = pl.pallas_call(
        functools.partial(body, S, C, D, heads, freqs),
        out_shape=(
            jax.ShapeDtypeStruct((count, width), bf),
            jax.ShapeDtypeStruct((n, padded, hd), f32),
            jax.ShapeDtypeStruct((n, rows, hd), f32),
        ),
        in_specs=[hbm, hbm, hbm, vmem, pl.BlockSpec(memory_space=pltpu.SMEM), hbm],
        out_specs=(vmem, vmem, vmem),
        scratch_shapes=[
            pltpu.VMEM((3, count, width), bf),
            pltpu.VMEM((freqs, width), f32),
            pltpu.VMEM((count, width), bf),
            pltpu.VMEM((heads, 2, C * count, hd), bf),
            pltpu.VMEM((heads, count, hd), bf),
            pltpu.VMEM((heads, count, hd), bf),
            pltpu.VMEM((heads, count, hd), bf),
            pltpu.VMEM((last, 3, C * count, hd), bf),
            pltpu.VMEM((2, width), f32),
            pltpu.VMEM((n, 8, hd), f32),
            pltpu.VMEM((padded, hd), f32),
            pltpu.VMEM((count, hd), f32),
            pltpu.VMEM((count, hd), f32),
            dma((5,)),
            dma((heads,)), dma((heads,)), dma((heads,)), dma((heads,)),
            dma, dma, dma, dma, dma((2,)), dma((2,)),
            dma((last,)), dma((last,)), dma((last,)), dma((last,)),
            pltpu.SemaphoreType.REGULAR, pltpu.SemaphoreType.REGULAR,
        ],
        compiler_params=pltpu.CompilerParams(
            collective_id=0, has_side_effects=True, vmem_limit_bytes=VMEM_LIMIT if C <= 2 else 60 << 20
        ),
    )(
        pin(jnp.moveaxis(qkv[0, 0], 1, 0)),
        pin(qk_gain[0]),
        pin(mod_weight[0]),
        pin(positions),
        timesteps,
        pin(cotangent[0, 0]),
    )
    attn_out, grad = pl.pallas_call(
        functools.partial(store, n, heads),
        out_shape=(
            jax.ShapeDtypeStruct((count, width), bf),
            jax.ShapeDtypeStruct((rows, width), f32),
        ),
        in_specs=[pl.BlockSpec(memory_space=pl.ANY), vmem, vmem],
        out_specs=(pl.BlockSpec(memory_space=pl.ANY), pl.BlockSpec(memory_space=pl.ANY)),
        scratch_shapes=[pltpu.VMEM((heads, rows, hd), f32), dma, dma((heads,))],
        compiler_params=pltpu.CompilerParams(vmem_limit_bytes=4 << 20),
    )(attn, chans, embs)
    return attn_out[None, None], grad[None]


def solution(mesh):
    sizes = mesh.shape
    return jax.shard_map(
        functools.partial(local, sizes["segment"], sizes["ctx"], sizes["dp"]),
        mesh=mesh,
        in_specs=(
            P("segment", "dp", "ctx", None, None),
            P("segment", None, None),
            P("segment", None, None),
            P("dp", "ctx"),
            P("segment", "dp"),
            P("segment", "dp", "ctx", None),
        ),
        out_specs=(P("segment", "dp", "ctx", None), P("segment", ("ctx", "dp"), None)),
        check_vma=False,
    )
```
